32 devices in a mesh: gx: 2 (over core), gy: 4 (over y, x), gz: 4 (over z).
Axes of the slice: x: 2, y: 2, z: 4, core: 2. Of those that a mesh axis runs over, the one named last changes fastest.
Arguments:
- flexibility: bfloat16 [4, 4, 4, 1536, 1536], P('gx', 'gy', 'gz'), may hold values from -3 to 3, as said below
- dual_load: float32 [4, 4, 4, 3, 256, 128], P('gx', 'gy', 'gz'), may hold values from -20 to 20
- coarse_load: float32 [4, 4, 4, 128], replicated, may hold values from -384 to 384
- glue: int32 [4, 4, 4, 3], replicated, may hold values 0 or 1
- floating_flag: int32 [4, 4, 4], replicated, may hold values 0 or 1
Outputs:
- multipliers: float32 [4, 4, 4, 3, 256, 128], P('gx', 'gy', 'gz')
- residual: float32 [4, 4, 4, 3, 256, 128], P('gx', 'gy', 'gz')
The draws below stay inside these ranges and needn't reach their ends.
Inputs may be any that keep to these rules, and one draw needn't show every extreme that they name: `flexibility`: for every subdomain the [1536, 1536] matrix is symmetric and positive definite.
All inputs are finite; a program needn't handle non-finite values.
Results may differ from the reference program's by a relative error of at most 0.015.
Values sent between devices are 32-bit elements; how exact they have to be, the bound alone decides.
A program may use at most 128 MiB of HBM per device.

```python
import math
import jax
import jax.numpy as jnp
from jax import lax

F = 256
R = 128
ITERS = 4
NX = 4
NY = 4
NZ = 4


def draw_flexibility(key, part):
    matrix_order = 6 * F
    subdomains = NX * NY * NZ
    key_scale = jax.random.fold_in(key, 11)
    key_noise = jax.random.fold_in(key, 12)
    log_low, log_high = (math.log(0.1), 0.0)
    log_scale = jax.random.uniform(key_scale, (subdomains, matrix_order), jnp.float32, log_low, log_high)
    identity = jnp.eye(matrix_order, dtype=jnp.float32)
    spread = 0.225 / math.sqrt(2.0 * matrix_order)

    def one_matrix(number_scale):
        number, row_scale = number_scale
        sub_key = jax.random.fold_in(key_noise, number)
        noise_draw = jnp.clip(jax.random.normal(sub_key, (matrix_order, matrix_order), jnp.float32), -4.0, 4.0)
        symmetric = (noise_draw + noise_draw.T) * spread
        root_scale = jnp.exp(0.5 * row_scale)
        return (root_scale[:, None] * (identity + symmetric) * root_scale[None, :]).astype(jnp.bfloat16)
    numbers = jnp.arange(subdomains, dtype=jnp.int32)
    stacked = lax.map(one_matrix, (numbers, log_scale))
    return stacked.reshape(NX, NY, NZ, matrix_order, matrix_order)


def draw_dual_load(key, part):
    full_shape = (NX, NY, NZ, 3, F, R)
    key_noise = jax.random.fold_in(key, 21)
    key_face = jax.random.fold_in(key, 22)
    position = (jnp.arange(NX, dtype=jnp.float32) / max(NX - 1, 1)).reshape(NX, 1, 1, 1, 1, 1)
    face_scale = jnp.exp(jax.random.uniform(key_face, (NX, NY, NZ, 3, 1, 1), jnp.float32, 0.0, math.log(10.0)))
    noise_draw = jnp.clip(jax.random.normal(key_noise, full_shape, jnp.float32), -4.0, 4.0)
    rising = 3.0 ** position
    return 0.05 * rising * face_scale * noise_draw


def touch_ends(drawn, key, smallest, high):
    spot = [jax.random.randint(jax.random.fold_in(key, axis), (), 0, length) for axis, length in enumerate(drawn.shape)]
    main_axis = drawn.shape.index(max(drawn.shape))
    next_to = spot[:main_axis] + [(spot[main_axis] + 1) % drawn.shape[main_axis]] + spot[main_axis + 1:]
    return drawn.at[tuple(spot)].set(smallest).at[tuple(next_to)].set(high)


def scatter_about(stream_key, extent, deviation, most, kind=jnp.bfloat16):
    entries = deviation * jax.random.normal(stream_key, extent, jnp.float32)
    return jnp.clip(entries, min=-most, max=most).astype(kind)


def setup_inputs(seed: int = 0) -> dict:
    key_of = jax.random.split(jax.random.key(seed), 6)
    flexibility = draw_flexibility(jax.random.fold_in(key_of[5], 71), 0)
    dual_load = draw_dual_load(jax.random.fold_in(key_of[5], 71), 0)
    coarse_load = scatter_about(key_of[2], (NX, NY, NZ, R), (F // 4), 384.0, jnp.float32)
    glue = touch_ends((jax.random.randint(key_of[3], (NX, NY, NZ, 3), 0, 4) < 3).astype(jnp.int32), jax.random.fold_in(key_of[3], 1), 0, 1)
    floating_flag = touch_ends((jax.random.randint(key_of[4], (NX, NY, NZ), 0, 256) < 255).astype(jnp.int32), jax.random.fold_in(key_of[4], 1), 0, 1)
    return {"flexibility": flexibility, "dual_load": dual_load, "coarse_load": coarse_load, "glue": glue, "floating_flag": floating_flag}


def shifted(values, dimension, toward):
    length = values.shape[dimension]
    widths = [(0, 0)] * values.ndim
    if toward > 0:
        widths[dimension] = (0, 1)
        return lax.slice_in_dim(jnp.pad(values, widths), 1, length + 1, axis=dimension)
    widths[dimension] = (1, 0)
    return lax.slice_in_dim(jnp.pad(values, widths), 0, length, axis=dimension)

def coupling(glue, floating_flag):
    grid_shape = floating_flag.shape
    active = []
    for dimension in range(3):
        coordinate = lax.broadcasted_iota(jnp.int32, grid_shape, dimension)
        inside = (coordinate < grid_shape[dimension] - 1).astype(jnp.int32)
        active.append(inside * glue[..., dimension])
    return (jnp.stack(active, axis=-1), floating_flag)

def coarse_matrix(active, floating):
    grid_shape = floating.shape
    total_count = grid_shape[0] * grid_shape[1] * grid_shape[2]
    strides = (grid_shape[1] * grid_shape[2], grid_shape[2], 1)
    support = 2.0 / float(grid_shape[0] * grid_shape[0])
    degree = jnp.zeros(grid_shape, jnp.int32)
    for dimension in range(3):
        degree = degree + active[..., dimension] + shifted(active[..., dimension], dimension, -1)
    flat_float = floating.reshape(total_count).astype(jnp.float32)
    diagonal = jnp.where(flat_float > 0, degree.reshape(total_count).astype(jnp.float32) + support, 1.0)
    row_index = lax.broadcasted_iota(jnp.int32, (total_count, total_count), 0)
    col_index = lax.broadcasted_iota(jnp.int32, (total_count, total_count), 1)
    matrix = jnp.where(row_index == col_index, diagonal[:, None], 0.0)
    for dimension in range(3):
        link_weight = (active[..., dimension] * floating * shifted(floating, dimension, 1)).reshape(total_count).astype(jnp.float32)
        upper_band = jnp.where(col_index == row_index + strides[dimension], link_weight[:, None], 0.0)
        matrix = matrix - upper_band - upper_band.T
    return matrix

def reference(flexibility, dual_load, coarse_load, glue, floating_flag):
    active_int, floating_int = coupling(glue, floating_flag)
    active = active_int.astype(jnp.float32)
    floating = floating_int.astype(jnp.float32)
    factor = jnp.linalg.cholesky(coarse_matrix(active_int, floating_int))
    mode_value = 1.0 / math.sqrt(F)
    subdomains = NX * NY * NZ
    face_mask = active[..., None, None]
    full_shape = (NX, NY, NZ, 3, F, R)

    def lower_faces(values):
        return jnp.stack([shifted(values[:, :, :, dimension], dimension, -1) for dimension in range(3)], axis=3)

    def coarse_solve(source):
        return jax.scipy.linalg.cho_solve((factor, True), source.reshape(subdomains, R)).reshape(NX, NY, NZ, R)

    def correction(amplitude):
        parts = [active[..., dimension, None] * mode_value * (amplitude - shifted(amplitude, dimension, 1)) for dimension in range(3)]
        return jnp.stack(parts, axis=3)[:, :, :, :, None, :]

    def project(values):
        source = mode_value * floating[..., None] * lax.optimization_barrier(jnp.sum(values - lower_faces(values), axis=(3, 4)))
        return values - correction(coarse_solve(source))
    matrices = flexibility.reshape(subdomains, 6 * F, 6 * F)

    def apply_one(matrix_load):
        return jnp.dot(matrix_load[0].astype(jnp.float32), matrix_load[1].astype(jnp.float32), precision=lax.Precision.HIGHEST)

    def operate(values, offset):
        below_values = lower_faces(values)
        face_list = []
        for dimension in range(3):
            face_list.append(-below_values[:, :, :, dimension])
            face_list.append(values[:, :, :, dimension])
        face_loads = jnp.stack(face_list, axis=3).astype(jnp.bfloat16).reshape(subdomains, 6 * F, R)
        traces = lax.map(apply_one, (matrices, face_loads)).reshape(NX, NY, NZ, 6, F, R)
        high_face = traces[:, :, :, 1::2] - offset
        partner = jnp.stack([shifted(traces[:, :, :, 2 * dimension], dimension, 1) for dimension in range(3)], axis=3)
        return face_mask * (high_face - partner)

    def inner_sums(left, right):
        return lax.optimization_barrier(jnp.sum(left * right, axis=(0, 1, 2, 3, 4)))
    multipliers = jnp.broadcast_to(correction(coarse_solve(floating[..., None] * coarse_load)), full_shape)
    residual = -operate(multipliers, dual_load)
    projected = project(residual)
    current = inner_sums(projected, projected)
    search = projected
    for iteration in range(ITERS):
        applied = operate(search, 0.0)
        step_size = current / inner_sums(search, applied)
        multipliers = multipliers + step_size * search
        residual = residual - step_size * applied
        projected = project(residual)
        renewed = inner_sums(projected, projected)
        if iteration + 1 < ITERS:
            search = projected + renewed / current * search
            current = renewed
    return (multipliers, projected)
```

```python
import functools
import math

import jax
import jax.numpy as jnp
from jax import lax
from jax.experimental import pallas as pl
from jax.experimental.pallas import tpu as pltpu
from jax.sharding import PartitionSpec as P

ITERS = 4
MESH = pl.DeviceIdType.MESH
AXES = ("gx", "gy", "gz")
HIGHEST = lax.Precision.HIGHEST


def shifted(values, dimension, toward):
    length = values.shape[dimension]
    widths = [(0, 0)] * values.ndim
    if toward > 0:
        widths[dimension] = (0, 1)
        return lax.slice_in_dim(jnp.pad(values, widths), 1, length + 1, axis=dimension)
    widths[dimension] = (1, 0)
    return lax.slice_in_dim(jnp.pad(values, widths), 0, length, axis=dimension)


def coupling(glue, floating_flag):
    grid_shape = floating_flag.shape
    active = []
    for dimension in range(3):
        coordinate = lax.broadcasted_iota(jnp.int32, grid_shape, dimension)
        inside = (coordinate < grid_shape[dimension] - 1).astype(jnp.int32)
        active.append(inside * glue[..., dimension])
    return (jnp.stack(active, axis=-1), floating_flag)


def coarse_matrix(active, floating):
    grid_shape = floating.shape
    total_count = grid_shape[0] * grid_shape[1] * grid_shape[2]
    strides = (grid_shape[1] * grid_shape[2], grid_shape[2], 1)
    support = 2.0 / float(grid_shape[0] * grid_shape[0])
    degree = jnp.zeros(grid_shape, jnp.int32)
    for dimension in range(3):
        degree = degree + active[..., dimension] + shifted(active[..., dimension], dimension, -1)
    flat_float = floating.reshape(total_count).astype(jnp.float32)
    diagonal = jnp.where(
        flat_float > 0, degree.reshape(total_count).astype(jnp.float32) + support, 1.0
    )
    row_index = lax.broadcasted_iota(jnp.int32, (total_count, total_count), 0)
    col_index = lax.broadcasted_iota(jnp.int32, (total_count, total_count), 1)
    matrix = jnp.where(row_index == col_index, diagonal[:, None], 0.0)
    for dimension in range(3):
        link_weight = (
            (active[..., dimension] * floating * shifted(floating, dimension, 1))
            .reshape(total_count)
            .astype(jnp.float32)
        )
        lower = jnp.where(row_index == col_index + strides[dimension], link_weight[None, :], 0.0)
        upper = jnp.where(col_index == row_index + strides[dimension], link_weight[:, None], 0.0)
        matrix = matrix - upper - lower
    return matrix


def dot32(left, right):
    return jnp.dot(left, right, precision=HIGHEST, preferred_element_type=jnp.float32)


def column_sums(values):
    return jnp.sum(values, axis=0, keepdims=True)


def kernel(
    counts,
    block_x,
    face,
    flex_hbm,
    dual_hbm,
    coarse_ref,
    mask_ref,
    matrix_ref,
    mult_ref,
    out_ref,
    flex,
    dual,
    inverse,
    projector,
    load,
    trace,
    other,
    search,
    resid,
    applied,
    source,
    gathered,
    flex_sem,
    dual_sem,
    send_sem,
    recv_sem,
    gsend_sem,
    grecv_sem,
):
    nx, ny, nz = counts
    me = [lax.axis_index(axis) for axis in AXES]
    order = (2, 3, 4, 5, 0, 1)
    cases = coarse_ref.shape[1]
    total = coarse_ref.shape[0]
    grid_x = nx * block_x
    mode = 1.0 / math.sqrt(face)
    support = 2.0 / float(grid_x * grid_x)
    block_rows = -(-(block_x + 3) // 8) * 8
    devices = nx * ny * nz

    def peer(axis, step):
        return lax.rem(me[axis] + step, counts[axis])

    def flex_copy(i, f):
        rows = pl.ds(f * face, face)
        return pltpu.make_async_copy(
            flex_hbm.at[i, rows], flex.at[i, rows], flex_sem.at[i * 6 + f]
        )

    dual_copy = pltpu.make_async_copy(dual_hbm, dual, dual_sem)
    for f in order:
        for i in range(block_x):
            flex_copy(i, f).start()
        if f == 2:
            dual_copy.start()

    other[...] = jnp.zeros_like(other)
    barrier = pltpu.get_barrier_semaphore()
    for axis in range(3):
        for step in range(1, counts[axis]):
            pl.semaphore_signal(
                barrier, inc=1, device_id={AXES[axis]: peer(axis, step)}, device_id_type=MESH
            )

    inverse[...] = matrix_ref[...]
    lane = lax.broadcasted_iota(jnp.int32, (total, total), 1)
    line = lax.broadcasted_iota(jnp.int32, (total, total), 0)
    lane_one = lax.broadcasted_iota(jnp.int32, (1, total), 1)

    def eliminate(k, carry):
        values = inverse[...]
        pivot_row = inverse[pl.ds(k, 1), :]
        pivot = jnp.sum(jnp.where(lane_one == k, pivot_row, 0.0), axis=1, keepdims=True)
        column = jnp.sum(jnp.where(lane == k, values, 0.0), axis=1, keepdims=True)
        scale = 1.0 / pivot
        scaled = jnp.where(lane_one == k, scale, pivot_row * scale)
        rest = jnp.where(lane == k, 0.0, values) - column * scaled
        inverse[...] = jnp.where(line == k, scaled, rest)
        return carry

    lax.fori_loop(0, total, eliminate, 0)

    faces = 6 * block_x
    row = lax.broadcasted_iota(jnp.int32, (faces, total), 0)
    col = lax.broadcasted_iota(jnp.int32, (faces, total), 1)
    own = jnp.zeros((faces, total), jnp.int32)
    near = jnp.zeros((faces, total), jnp.int32)
    strides = (ny * nz, nz, 1)
    for i in range(block_x):
        here = ((me[0] * block_x + i) * ny + me[1]) * nz + me[2]
        for f in range(6):
            there = here + (strides[f // 2] if f % 2 else -strides[f // 2])
            own = jnp.where(row == i * 6 + f, here, own)
            near = jnp.where(row == i * 6 + f, there, near)
    difference = jnp.where(col == own, mode, 0.0) - jnp.where(col == near, mode, 0.0)
    difference = difference * mask_ref[0:faces, 0:1]
    projector[...] = dot32(difference, inverse[...])

    begin = dot32(projector[...], coarse_ref[...])
    resid[...] = jnp.zeros_like(resid)
    mult_ref[...] = jnp.zeros_like(mult_ref)
    source[...] = jnp.zeros_like(source)
    for i in range(block_x):
        for f in range(6):
            values = jnp.broadcast_to(begin[i * 6 + f : i * 6 + f + 1], (face, cases))
            search[i, f] = values
            load[i, f * face : (f + 1) * face] = values.astype(jnp.bfloat16)

    pl.semaphore_wait(barrier, sum(counts) - 3)

    def remote(i, f):
        if f >= 2:
            return True
        return i == 0 if f == 0 else i == block_x - 1

    def has_near(f):
        return me[f // 2] < counts[f // 2] - 1 if f % 2 else me[f // 2] > 0

    def face_copy(i, f):
        axis = f // 2
        target = me[axis] + (1 if f % 2 else -1)
        into = i
        if axis == 0:
            into = 0 if f % 2 else block_x - 1
        return pltpu.make_async_remote_copy(
            src_ref=trace.at[i, f],
            dst_ref=other.at[into, f ^ 1],
            send_sem=send_sem.at[i * 6 + f],
            recv_sem=recv_sem.at[into * 6 + (f ^ 1)],
            device_id={AXES[axis]: target},
            device_id_type=MESH,
        )

    def arrival(i, f):
        axis = f // 2
        return pltpu.make_async_remote_copy(
            src_ref=trace.at[i, f],
            dst_ref=other.at[i, f],
            send_sem=send_sem.at[i * 6 + f],
            recv_sem=recv_sem.at[i * 6 + f],
            device_id={AXES[axis]: me[axis] + (1 if f % 2 else -1)},
            device_id_type=MESH,
        )

    spans = (devices, ny * nz, nz, 1)
    place = (me[0] * ny + me[1]) * nz + me[2]

    def gather(slot):
        for axis in (2, 1, 0):
            width = spans[axis + 1]
            start = lax.div(place, width) * width
            rows = pl.ds(pl.multiple_of(start * block_rows, 8), width * block_rows)
            copies = []
            for step in range(1, counts[axis]):
                copy = pltpu.make_async_remote_copy(
                    src_ref=gathered.at[slot, rows],
                    dst_ref=gathered.at[slot, rows],
                    send_sem=gsend_sem.at[slot, axis, step],
                    recv_sem=grecv_sem.at[slot, axis, step],
                    device_id={AXES[axis]: peer(axis, step)},
                    device_id_type=MESH,
                )
                copy.start()
                copies.append(copy)
            for copy in copies:
                copy.wait()

    def iterate(it, carry):
        current, squared = carry
        slot = lax.rem(it, 2)
        first = it == 0
        last = it == ITERS

        for f in order:
            for i in range(block_x):

                @pl.when(first)
                def _():
                    flex_copy(i, f).wait()

                trace[i, f] = jnp.dot(
                    flex[i, f * face : (f + 1) * face, :],
                    load[i],
                    preferred_element_type=jnp.float32,
                )
                if f % 2:

                    @pl.when(first)
                    def _():
                        if f == 3 and i == 0:
                            dual_copy.wait()
                        trace[i, f] = trace[i, f] - dual[i, f // 2]

                if remote(i, f):

                    @pl.when(has_near(f))
                    def _():
                        face_copy(i, f).start()

        sums = [jnp.zeros((1, cases), jnp.float32) for _ in range(3)]
        sources = [jnp.zeros((1, cases), jnp.float32) for _ in range(block_x)]
        for f in (0, 1, 2, 3, 4, 5):
            for i in range(block_x):
                if remote(i, f):

                    @pl.when(has_near(f))
                    def _():
                        arrival(i, f).wait_recv()

                    partner = other[i, f]
                else:
                    partner = trace[i + (1 if f % 2 else -1), f ^ 1]
                row_of = i * 6 + f
                values = mask_ref[row_of : row_of + 1, :] * (trace[i, f] - partner)
                applied[i, f] = values
                sources[i] = sources[i] + column_sums(values)
                if f % 2:
                    sums[0] = sums[0] + column_sums(search[i, f] * values)
                    sums[1] = sums[1] + column_sums(resid[i, f] * values)
                    sums[2] = sums[2] + column_sums(values * values)
        sources = [
            sources[i] * mask_ref[faces + i : faces + i + 1, :] for i in range(block_x)
        ]
        lines = sources + sums
        lines = lines + [jnp.zeros((1, cases), jnp.float32)] * (block_rows - len(lines))
        gathered[slot, pl.ds(pl.multiple_of(place * block_rows, 8), block_rows)] = (
            jnp.concatenate(lines, axis=0)
        )
        gather(slot)

        totals = [
            column_sums(gathered[slot, pl.ds(block_x + j, devices, stride=block_rows), :])
            for j in range(3)
        ]
        step = jnp.where(first, 1.0, current / totals[0])
        plane = ny * nz
        for gx in range(nx):
            for i in range(block_x):
                at = (gx * block_x + i) * plane
                source[at : at + plane] = (
                    source[at : at + plane]
                    - step
                    * gathered[slot, pl.ds(gx * plane * block_rows + i, plane, stride=block_rows), :]
                )
        amplitude = dot32(inverse[...], source[...])
        spread = dot32(projector[...], source[...])
        squared = squared - 2.0 * step * totals[1] + step * step * totals[2]
        removed = column_sums(source[...] * amplitude)
        removed = removed + support * column_sums(amplitude * amplitude)
        renewed = squared - removed
        ratio = jnp.where(jnp.logical_or(first, last), 0.0, renewed / current)

        for i in range(block_x):
            for f in range(6):
                row_of = i * 6 + f
                old = search[i, f]
                left = resid[i, f] - step * applied[i, f]
                resid[i, f] = left
                fresh = (left - spread[row_of : row_of + 1]) + ratio * old
                search[i, f] = fresh
                load[i, f * face : (f + 1) * face] = fresh.astype(jnp.bfloat16)
                if f % 2:
                    mult_ref[i, f // 2] = mult_ref[i, f // 2] + step * old
                if remote(i, f):

                    @pl.when(has_near(f))
                    def _():
                        face_copy(i, f).wait_send()

        return renewed, squared

    zero = jnp.zeros((1, cases), jnp.float32)
    lax.fori_loop(0, ITERS + 1, iterate, (zero, zero))
    for i in range(block_x):
        for d in range(3):
            out_ref[i, d] = search[i, 2 * d + 1]


def per_device(counts, flexibility, dual_load, coarse_load, glue, floating_flag):
    block_x, block_y, block_z = dual_load.shape[:3]
    face, cases = dual_load.shape[4:]
    assert block_y == 1 and block_z == 1
    grid_x, grid_y, grid_z = floating_flag.shape
    total = grid_x * grid_y * grid_z
    nx, ny, nz = counts
    start = (lax.axis_index("gx") * block_x, lax.axis_index("gy"), lax.axis_index("gz"))
    active_int, floating_int = coupling(glue, floating_flag)
    matrix = coarse_matrix(active_int, floating_int)
    floating = floating_int.astype(jnp.float32)
    columns = []
    for d in range(3):
        columns.append(shifted(active_int[..., d], d, -1).astype(jnp.float32))
        columns.append(active_int[..., d].astype(jnp.float32))
    columns.append(floating / math.sqrt(face))
    table = lax.dynamic_slice(
        jnp.stack(columns, axis=-1), start + (0,), (block_x, 1, 1, 7)
    ).reshape(block_x, 7)
    masks = jnp.concatenate([table[:, :6].reshape(block_x * 6), table[:, 6]])
    rows = -(-(block_x * 7) // 8) * 8
    masks = jnp.pad(masks, (0, rows - block_x * 7))
    masks = jnp.broadcast_to(masks[:, None], (rows, cases))
    coarse = (floating[..., None] * coarse_load).reshape(total, cases)
    block_rows = -(-(block_x + 3) // 8) * 8
    devices = nx * ny * nz
    fields = (block_x, 6, face, cases)
    vmem = pl.BlockSpec(memory_space=pltpu.VMEM)
    hbm = pl.BlockSpec(memory_space=pl.ANY)
    out = jax.ShapeDtypeStruct((block_x, 3, face, cases), jnp.float32)
    most = max(counts)
    mult, resid = pl.pallas_call(
        functools.partial(kernel, counts, block_x, face),
        out_shape=(out, out),
        in_specs=[hbm, hbm, vmem, vmem, vmem],
        out_specs=(vmem, vmem),
        scratch_shapes=[
            pltpu.VMEM((block_x, 6 * face, 6 * face), jnp.bfloat16),
            pltpu.VMEM((block_x, 3, face, cases), jnp.float32),
            pltpu.VMEM((total, total), jnp.float32),
            pltpu.VMEM((6 * block_x, total), jnp.float32),
            pltpu.VMEM((block_x, 6 * face, cases), jnp.bfloat16),
            pltpu.VMEM(fields, jnp.float32),
            pltpu.VMEM(fields, jnp.float32),
            pltpu.VMEM(fields, jnp.float32),
            pltpu.VMEM(fields, jnp.float32),
            pltpu.VMEM(fields, jnp.float32),
            pltpu.VMEM((total, cases), jnp.float32),
            pltpu.VMEM((2, devices * block_rows, cases), jnp.float32),
            pltpu.SemaphoreType.DMA((6 * block_x,)),
            pltpu.SemaphoreType.DMA,
            pltpu.SemaphoreType.DMA((6 * block_x,)),
            pltpu.SemaphoreType.DMA((6 * block_x,)),
            pltpu.SemaphoreType.DMA((2, 3, most)),
            pltpu.SemaphoreType.DMA((2, 3, most)),
        ],
        compiler_params=pltpu.CompilerParams(collective_id=0, has_side_effects=True),
        name="feti_cg",
    )(
        flexibility.reshape(block_x, 6 * face, 6 * face),
        dual_load.reshape(block_x, 3, face, cases),
        coarse,
        masks,
        matrix,
    )
    shape = dual_load.shape
    return mult.reshape(shape), resid.reshape(shape)


def solution(mesh):
    counts = tuple(mesh.shape[axis] for axis in AXES)
    return jax.shard_map(
        functools.partial(per_device, counts),
        mesh=mesh,
        in_specs=(
            P("gx", "gy", "gz", None, None),
            P("gx", "gy", "gz", None, None, None),
            P(),
            P(),
            P(),
        ),
        out_specs=(P("gx", "gy", "gz", None, None, None), P("gx", "gy", "gz", None, None, None)),
        check_vma=False,
    )
```

```python
import functools
import math

import jax
import jax.numpy as jnp
from jax import lax
from jax.experimental import pallas as pl
from jax.experimental.pallas import tpu as pltpu
from jax.sharding import PartitionSpec as P

ITERS = 4
MESH = pl.DeviceIdType.MESH
AXES = ("gx", "gy", "gz")
HIGHEST = lax.Precision.HIGHEST


def dot32(left, right):
    return jnp.dot(left, right, precision=HIGHEST, preferred_element_type=jnp.float32)


def column_sums(values):
    return jnp.sum(values, axis=0, keepdims=True)


def kernel(
    counts,
    block_x,
    face,
    flex_hbm,
    dual_hbm,
    coarse_ref,
    pack_ref,
    mult_ref,
    out_ref,
    begin_ref,
    spread_ref,
    flex,
    dual,
    inverse,
    projector,
    masks,
    load,
    trace,
    other,
    fresh,
    search,
    resid,
    applied,
    source,
    applied_source,
    gathered,
    face_sums,
    near_sums,
    flex_sem,
    dual_sem,
    send_sem,
    recv_sem,
    ssend_sem,
    srecv_sem,
    gsend_sem,
    grecv_sem,
):
    nx, ny, nz = counts
    me = [lax.axis_index(axis) for axis in AXES]
    cases = coarse_ref.shape[1]
    total = coarse_ref.shape[0]
    grid = (nx * block_x, ny, nz)
    mode = 1.0 / math.sqrt(face)
    support = 2.0 / float(grid[0] * grid[0])
    block_rows = -(-(block_x + 4) // 8) * 8
    devices = nx * ny * nz
    faces = 6 * block_x
    strides = (ny * nz, nz, 1)

    def peer(axis, step):
        return lax.rem(me[axis] + step, counts[axis])

    def flex_copy(i, f):
        rows = pl.ds(f * face, face)
        return pltpu.make_async_copy(
            flex_hbm.at[i, rows], flex.at[i, rows], flex_sem.at[i * 6 + f]
        )

    dual_copy = pltpu.make_async_copy(dual_hbm, dual, dual_sem)
    for f in (2, 3, 4, 5, 0, 1):
        for i in range(block_x):
            flex_copy(i, f).start()
        if f == 2:
            dual_copy.start()

    other[...] = jnp.zeros_like(other)
    near_sums[...] = jnp.zeros_like(near_sums)
    barrier = pltpu.get_barrier_semaphore()
    for axis in range(3):
        for step in range(1, counts[axis]):
            pl.semaphore_signal(
                barrier, inc=1, device_id={AXES[axis]: peer(axis, step)}, device_id_type=MESH
            )

    lane = lax.broadcasted_iota(jnp.int32, (total, total), 1)
    line = lax.broadcasted_iota(jnp.int32, (total, total), 0)
    lane_one = lax.broadcasted_iota(jnp.int32, (1, total), 1)
    tall = lax.broadcasted_iota(jnp.int32, (total, cases), 0)
    floating = pack_ref[3 * total : 4 * total, :]

    def pick(choice, values):
        return jnp.dot(choice, values, preferred_element_type=jnp.float32)

    degree = jnp.zeros((total, cases), jnp.float32)
    bands = jnp.zeros((total, total), jnp.float32)
    for d in range(3):
        place_d = lax.rem(lax.div(tall, strides[d]), grid[d])
        active = jnp.where(place_d < grid[d] - 1, pack_ref[d * total : (d + 1) * total, :], 0.0)
        above = jnp.where(lane == line + strides[d], 1.0, 0.0)
        below = jnp.where(lane == line - strides[d], 1.0, 0.0)
        active_below = pick(below, active)
        degree = degree + active + active_below
        link_above = active * floating * pick(above, floating)
        link_below = active_below * floating * pick(below, floating)
        bands = bands + above * link_above[:, 0:1] + below * link_below[:, 0:1]
    diagonal = jnp.where(floating > 0.0, degree + support, 1.0)
    inverse[...] = jnp.where(lane == line, diagonal[:, 0:1], 0.0) - bands

    def eliminate(k, carry):
        values = inverse[...]
        pivot_row = inverse[pl.ds(k, 1), :]
        pivot = jnp.sum(jnp.where(lane_one == k, pivot_row, 0.0), axis=1, keepdims=True)
        column = jnp.sum(jnp.where(lane == k, values, 0.0), axis=1, keepdims=True)
        scale = 1.0 / pivot
        scaled = jnp.where(lane_one == k, scale, pivot_row * scale)
        rest = jnp.where(lane == k, 0.0, values) - column * scaled
        inverse[...] = jnp.where(line == k, scaled, rest)
        return carry

    lax.fori_loop(0, total, eliminate, 0)

    mask_rows = masks.shape[0]
    wide = lax.broadcasted_iota(jnp.int32, (mask_rows, 4 * total), 0)
    across = lax.broadcasted_iota(jnp.int32, (mask_rows, 4 * total), 1)
    row = lax.broadcasted_iota(jnp.int32, (faces, total), 0)
    col = lax.broadcasted_iota(jnp.int32, (faces, total), 1)
    own = jnp.zeros((faces, total), jnp.int32)
    near = jnp.zeros((faces, total), jnp.int32)
    chosen = jnp.full((mask_rows, 4 * total), -1, jnp.int32)
    for i in range(block_x):
        spot = (me[0] * block_x + i, me[1], me[2])
        here = (spot[0] * ny + spot[1]) * nz + spot[2]
        for f in range(6):
            d = f // 2
            there = here + (strides[d] if f % 2 else -strides[d])
            own = jnp.where(row == i * 6 + f, here, own)
            near = jnp.where(row == i * 6 + f, there, near)
            if f % 2:
                entry = jnp.where(spot[d] < grid[d] - 1, d * total + here, -1)
            else:
                entry = jnp.where(spot[d] > 0, d * total + there, -1)
            chosen = jnp.where(wide == i * 6 + f, entry, chosen)
        chosen = jnp.where(wide == faces + i, 3 * total + here, chosen)
    masks[...] = pick(jnp.where(across == chosen, 1.0, 0.0), pack_ref[...])
    difference = jnp.where(col == own, mode, 0.0) - jnp.where(col == near, mode, 0.0)
    difference = difference * masks[0:faces, 0:1]
    projector[...] = dot32(difference, inverse[...])

    begin = dot32(projector[...], floating * coarse_ref[...])
    search[...] = jnp.zeros_like(search)
    applied[...] = jnp.zeros_like(applied)
    resid[...] = jnp.zeros_like(resid)
    mult_ref[...] = jnp.zeros_like(mult_ref)
    source[...] = jnp.zeros_like(source)
    applied_source[...] = jnp.zeros_like(applied_source)
    face_sums[...] = jnp.zeros_like(face_sums)
    for i in range(block_x):
        for f in range(6):
            line_f = begin[i * 6 + f : i * 6 + f + 1]
            values = jnp.broadcast_to(line_f, (face, cases))
            fresh[i, f] = values
            load[i, f * face : (f + 1) * face] = values.astype(jnp.bfloat16)
            if f % 2:
                begin_ref[i, f // 2] = line_f

    pl.semaphore_wait(barrier, sum(counts) - 3)

    def remote(i, f):
        if f >= 2:
            return True
        return i == 0 if f == 0 else i == block_x - 1

    def has_near(f):
        return me[f // 2] < counts[f // 2] - 1 if f % 2 else me[f // 2] > 0

    def neighbour(f):
        return {AXES[f // 2]: me[f // 2] + (1 if f % 2 else -1)}

    def face_copy(slot, i, f, into):
        return pltpu.make_async_remote_copy(
            src_ref=trace.at[i, f],
            dst_ref=other.at[slot, into, f ^ 1],
            send_sem=send_sem.at[i * 6 + f],
            recv_sem=recv_sem.at[slot, into * 6 + (f ^ 1)],
            device_id=neighbour(f),
            device_id_type=MESH,
        )

    def send_face(slot, i, f):
        into = i
        if f < 2:
            into = 0 if f % 2 else block_x - 1
        return face_copy(slot, i, f, into)

    def arrival(slot, i, f):
        return pltpu.make_async_remote_copy(
            src_ref=trace.at[i, f],
            dst_ref=other.at[slot, i, f],
            send_sem=send_sem.at[i * 6 + f],
            recv_sem=recv_sem.at[slot, i * 6 + f],
            device_id=neighbour(f),
            device_id_type=MESH,
        )

    def sum_copy(f, g):
        return pltpu.make_async_remote_copy(
            src_ref=face_sums.at[f],
            dst_ref=near_sums.at[g],
            send_sem=ssend_sem.at[f],
            recv_sem=srecv_sem.at[g],
            device_id=neighbour(f),
            device_id_type=MESH,
        )

    spans = (devices, ny * nz, nz, 1)
    place = (me[0] * ny + me[1]) * nz + me[2]

    def gather(slot):
        for axis in (2, 1, 0):
            width = spans[axis + 1]
            start = lax.div(place, width) * width
            rows = pl.ds(pl.multiple_of(start * block_rows, 8), width * block_rows)
            copies = []
            for step in range(1, counts[axis]):
                copy = pltpu.make_async_remote_copy(
                    src_ref=gathered.at[slot, rows],
                    dst_ref=gathered.at[slot, rows],
                    send_sem=gsend_sem.at[slot, axis, step],
                    recv_sem=grecv_sem.at[slot, axis, step],
                    device_id={AXES[axis]: peer(axis, step)},
                    device_id_type=MESH,
                )
                copy.start()
                copies.append(copy)
            for copy in copies:
                copy.wait()

    def iterate(it, carry):
        before, curve = carry
        slot = lax.rem(it, 2)
        first = it == 0

        ww = jnp.zeros((1, cases), jnp.float32)
        wq = jnp.zeros((1, cases), jnp.float32)
        wt = jnp.zeros((1, cases), jnp.float32)
        pt = jnp.zeros((1, cases), jnp.float32)
        for d in (1, 2, 0):
            for f in (2 * d, 2 * d + 1):
                for i in range(block_x):

                    @pl.when(first)
                    def _():
                        flex_copy(i, f).wait()

                    trace[i, f] = jnp.dot(
                        flex[i, f * face : (f + 1) * face, :],
                        load[i],
                        preferred_element_type=jnp.float32,
                    )
                    if f % 2:

                        @pl.when(first)
                        def _():
                            if f == 3 and i == 0:
                                dual_copy.wait()
                            trace[i, f] = trace[i, f] - dual[i, f // 2]

                    face_sums[f, i : i + 1] = column_sums(trace[i, f])

                @pl.when(has_near(f))
                def _():
                    sum_copy(f, f ^ 1).start()
                    for i in range(block_x):
                        if remote(i, f):
                            send_face(slot, i, f).start()

        for f in range(6):
            for i in range(block_x):
                values = trace[i, f]
                now = fresh[i, f]
                wt = wt + column_sums(now * values)
                pt = pt + column_sums(search[i, f] * values)
                if f % 2:
                    ww = ww + column_sums(now * now)
                    wq = wq + column_sums(now * applied[i, f])

        sources = [jnp.zeros((1, cases), jnp.float32) for _ in range(block_x)]
        for f in (2, 3, 4, 5, 0, 1):

            @pl.when(has_near(f))
            def _():
                sum_copy(f, f).wait_recv()

            for i in range(block_x):
                step = 1 if f % 2 else -1
                if f >= 2:
                    partner = near_sums[f, i : i + 1]
                elif remote(i, f):
                    k = block_x - 1 - i
                    partner = near_sums[f, k : k + 1]
                else:
                    partner = face_sums[f ^ 1, i + step : i + step + 1]
                row_of = i * 6 + f
                sources[i] = sources[i] + masks[row_of : row_of + 1, :] * (
                    face_sums[f, i : i + 1] - partner
                )
        lines = [
            sources[i] * (mode * masks[faces + i : faces + i + 1, :]) for i in range(block_x)
        ]
        lines = lines + [ww, wt, wq, pt]
        lines = lines + [jnp.zeros((1, cases), jnp.float32)] * (block_rows - len(lines))
        gathered[slot, pl.ds(pl.multiple_of(place * block_rows, 8), block_rows)] = (
            jnp.concatenate(lines, axis=0)
        )
        gather(slot)

        ww, wt, wq, pt = [
            column_sums(gathered[slot, pl.ds(block_x + j, devices, stride=block_rows), :])
            for j in range(4)
        ]
        ratio = jnp.where(it <= 1, 0.0, ww / before)
        curve = wt + ratio * (wq + pt) + ratio * ratio * curve
        length = jnp.where(first, 1.0, ww / curve)
        plane = ny * nz
        for gx in range(nx):
            for i in range(block_x):
                at = (gx * block_x + i) * plane
                part = (
                    gathered[slot, pl.ds(gx * plane * block_rows + i, plane, stride=block_rows), :]
                    + ratio * applied_source[at : at + plane]
                )
                applied_source[at : at + plane] = part
                source[at : at + plane] = source[at : at + plane] - length * part
        spread = dot32(projector[...], source[...])
        moved = jnp.where(first, 0.0, length)

        for f in (0, 1, 4, 5, 2, 3):
            for i in range(block_x):
                if remote(i, f):

                    @pl.when(has_near(f))
                    def _():
                        arrival(slot, i, f).wait_recv()
                        send_face(slot, i, f).wait_send()

                    partner = other[slot, i, f]
                else:
                    partner = trace[i + (1 if f % 2 else -1), f ^ 1]
                row_of = i * 6 + f
                jump = masks[row_of : row_of + 1, :] * (trace[i, f] - partner)
                product = jump + ratio * applied[i, f]
                applied[i, f] = product
                toward = fresh[i, f] + ratio * search[i, f]
                search[i, f] = toward
                if f % 2:
                    mult_ref[i, f // 2] = mult_ref[i, f // 2] + moved * toward
                left = resid[i, f] - length * product
                resid[i, f] = left
                renewed = left - spread[row_of : row_of + 1]
                fresh[i, f] = renewed
                load[i, f * face : (f + 1) * face] = renewed.astype(jnp.bfloat16)
                if f % 2:
                    spread_ref[i, f // 2] = spread[row_of : row_of + 1]

            @pl.when(has_near(f))
            def _():
                sum_copy(f, f ^ 1).wait_send()

        return ww, curve

    zero = jnp.zeros((1, cases), jnp.float32)
    lax.fori_loop(0, ITERS + 1, iterate, (zero, zero))
    for i in range(block_x):
        for d in range(3):
            out_ref[i, d] = resid[i, 2 * d + 1]


def per_device(counts, flexibility, dual_load, coarse_load, glue, floating_flag):
    block_x, block_y, block_z = dual_load.shape[:3]
    face, cases = dual_load.shape[4:]
    assert block_y == 1 and block_z == 1
    grid_x, grid_y, grid_z = floating_flag.shape
    total = grid_x * grid_y * grid_z
    nx, ny, nz = counts
    packed = jnp.concatenate([jnp.moveaxis(glue, 3, 0).reshape(3 * total), floating_flag.reshape(total)])
    packed = jnp.broadcast_to(packed.astype(jnp.float32)[:, None], (4 * total, cases))
    coarse = coarse_load.reshape(total, cases)
    block_rows = -(-(block_x + 4) // 8) * 8
    sum_rows = -(-block_x // 8) * 8
    mask_rows = -(-(block_x * 7) // 8) * 8
    devices = nx * ny * nz
    fields = (block_x, 6, face, cases)
    vmem = pl.BlockSpec(memory_space=pltpu.VMEM)
    hbm = pl.BlockSpec(memory_space=pl.ANY)
    out = jax.ShapeDtypeStruct((block_x, 3, face, cases), jnp.float32)
    most = max(counts)
    small = jax.ShapeDtypeStruct((block_x, 3, 1, cases), jnp.float32)
    mult, resid, begin, spread = pl.pallas_call(
        functools.partial(kernel, counts, block_x, face),
        out_shape=(out, out, small, small),
        in_specs=[hbm, hbm, vmem, vmem],
        out_specs=(vmem, vmem, vmem, vmem),
        scratch_shapes=[
            pltpu.VMEM((block_x, 6 * face, 6 * face), jnp.bfloat16),
            pltpu.VMEM((block_x, 3, face, cases), jnp.float32),
            pltpu.VMEM((total, total), jnp.float32),
            pltpu.VMEM((6 * block_x, total), jnp.float32),
            pltpu.VMEM((mask_rows, cases), jnp.float32),
            pltpu.VMEM((block_x, 6 * face, cases), jnp.bfloat16),
            pltpu.VMEM(fields, jnp.float32),
            pltpu.VMEM((2,) + fields, jnp.float32),
            pltpu.VMEM(fields, jnp.float32),
            pltpu.VMEM(fields, jnp.float32),
            pltpu.VMEM(fields, jnp.float32),
            pltpu.VMEM(fields, jnp.float32),
            pltpu.VMEM((total, cases), jnp.float32),
            pltpu.VMEM((total, cases), jnp.float32),
            pltpu.VMEM((2, devices * block_rows, cases), jnp.float32),
            pltpu.VMEM((6, sum_rows, cases), jnp.float32),
            pltpu.VMEM((6, sum_rows, cases), jnp.float32),
            pltpu.SemaphoreType.DMA((6 * block_x,)),
            pltpu.SemaphoreType.DMA,
            pltpu.SemaphoreType.DMA((6 * block_x,)),
            pltpu.SemaphoreType.DMA((2, 6 * block_x)),
            pltpu.SemaphoreType.DMA((6,)),
            pltpu.SemaphoreType.DMA((6,)),
            pltpu.SemaphoreType.DMA((2, 3, most)),
            pltpu.SemaphoreType.DMA((2, 3, most)),
        ],
        compiler_params=pltpu.CompilerParams(collective_id=0, has_side_effects=True),
        name="feti_cg",
    )(
        flexibility.reshape(block_x, 6 * face, 6 * face),
        dual_load.reshape(block_x, 3, face, cases),
        coarse,
        packed,
    )
    shape = dual_load.shape
    return (mult + begin).reshape(shape), (resid - spread).reshape(shape)


def solution(mesh):
    counts = tuple(mesh.shape[axis] for axis in AXES)
    return jax.shard_map(
        functools.partial(per_device, counts),
        mesh=mesh,
        in_specs=(
            P("gx", "gy", "gz", None, None),
            P("gx", "gy", "gz", None, None, None),
            P(),
            P(),
            P(),
        ),
        out_specs=(P("gx", "gy", "gz", None, None, None), P("gx", "gy", "gz", None, None, None)),
        check_vma=False,
    )
```

```python
import functools
import math

import jax
import jax.numpy as jnp
from jax import lax
from jax.experimental import pallas as pl
from jax.experimental.pallas import tpu as pltpu
from jax.sharding import PartitionSpec as P

ITERS = 4
MESH = pl.DeviceIdType.MESH
AXES = ("gx", "gy", "gz")
HIGHEST = lax.Precision.HIGHEST


def dot32(left, right):
    return jnp.dot(left, right, precision=HIGHEST, preferred_element_type=jnp.float32)


def column_sums(values):
    return jnp.sum(values, axis=0, keepdims=True)


def kernel(
    counts,
    block_x,
    face,
    flex_hbm,
    dual_hbm,
    coarse_ref,
    pack_ref,
    mult_ref,
    out_ref,
    begin_ref,
    spread_ref,
    flex,
    dual,
    inverse,
    projector,
    masks,
    load,
    trace,
    other,
    fresh,
    search,
    resid,
    applied,
    source,
    applied_source,
    gathered,
    face_sums,
    near_sums,
    flex_sem,
    dual_sem,
    send_sem,
    recv_sem,
    ssend_sem,
    srecv_sem,
    gsend_sem,
    grecv_sem,
):
    nx, ny, nz = counts
    me = [lax.axis_index(axis) for axis in AXES]
    cases = coarse_ref.shape[1]
    total = coarse_ref.shape[0]
    grid = (nx * block_x, ny, nz)
    mode = 1.0 / math.sqrt(face)
    support = 2.0 / float(grid[0] * grid[0])
    block_rows = -(-(block_x + 4) // 8) * 8
    devices = nx * ny * nz
    faces = 6 * block_x
    strides = (ny * nz, nz, 1)

    def peer(axis, step):
        return lax.rem(me[axis] + step, counts[axis])

    def plane_peers():
        found = []
        for step_y in range(ny):
            for step_z in range(nz):
                if step_y or step_z:
                    target = {"gy": peer(1, step_y), "gz": peer(2, step_z)}
                    found.append((step_y * nz + step_z, target))
        return found

    def line_peers():
        return [(step, {"gx": peer(0, step)}) for step in range(1, nx)]

    def flex_copy(i, f):
        rows = pl.ds(f * face, face)
        return pltpu.make_async_copy(
            flex_hbm.at[i, rows], flex.at[i, rows], flex_sem.at[i * 6 + f]
        )

    dual_copy = pltpu.make_async_copy(dual_hbm, dual, dual_sem)
    for f in (2, 3, 4, 5, 0, 1):
        for i in range(block_x):
            flex_copy(i, f).start()
        if f == 2:
            dual_copy.start()

    other[...] = jnp.zeros_like(other)
    near_sums[...] = jnp.zeros_like(near_sums)
    barrier = pltpu.get_barrier_semaphore()
    for target in plane_peers() + line_peers():
        pl.semaphore_signal(barrier, inc=1, device_id=target[1], device_id_type=MESH)

    lane = lax.broadcasted_iota(jnp.int32, (total, total), 1)
    line = lax.broadcasted_iota(jnp.int32, (total, total), 0)
    lane_one = lax.broadcasted_iota(jnp.int32, (1, total), 1)
    tall = lax.broadcasted_iota(jnp.int32, (total, cases), 0)
    floating = pack_ref[3 * total : 4 * total, :]

    def pick(choice, values):
        return jnp.dot(choice, values, preferred_element_type=jnp.float32)

    degree = jnp.zeros((total, cases), jnp.float32)
    bands = jnp.zeros((total, total), jnp.float32)
    for d in range(3):
        place_d = lax.rem(lax.div(tall, strides[d]), grid[d])
        active = jnp.where(place_d < grid[d] - 1, pack_ref[d * total : (d + 1) * total, :], 0.0)
        above = jnp.where(lane == line + strides[d], 1.0, 0.0)
        below = jnp.where(lane == line - strides[d], 1.0, 0.0)
        active_below = pick(below, active)
        degree = degree + active + active_below
        link_above = active * floating * pick(above, floating)
        link_below = active_below * floating * pick(below, floating)
        bands = bands + above * link_above[:, 0:1] + below * link_below[:, 0:1]
    diagonal = jnp.where(floating > 0.0, degree + support, 1.0)
    inverse[...] = jnp.where(lane == line, diagonal[:, 0:1], 0.0) - bands

    def eliminate(k, carry):
        values = inverse[...]
        pivot_row = inverse[pl.ds(k, 1), :]
        pivot = jnp.sum(jnp.where(lane_one == k, pivot_row, 0.0), axis=1, keepdims=True)
        column = jnp.sum(jnp.where(lane == k, values, 0.0), axis=1, keepdims=True)
        scale = 1.0 / pivot
        scaled = jnp.where(lane_one == k, scale, pivot_row * scale)
        rest = jnp.where(lane == k, 0.0, values) - column * scaled
        inverse[...] = jnp.where(line == k, scaled, rest)
        return carry

    lax.fori_loop(0, total, eliminate, 0)

    mask_rows = masks.shape[0]
    wide = lax.broadcasted_iota(jnp.int32, (mask_rows, 4 * total), 0)
    across = lax.broadcasted_iota(jnp.int32, (mask_rows, 4 * total), 1)
    row = lax.broadcasted_iota(jnp.int32, (faces, total), 0)
    col = lax.broadcasted_iota(jnp.int32, (faces, total), 1)
    own = jnp.zeros((faces, total), jnp.int32)
    near = jnp.zeros((faces, total), jnp.int32)
    chosen = jnp.full((mask_rows, 4 * total), -1, jnp.int32)
    for i in range(block_x):
        spot = (me[0] * block_x + i, me[1], me[2])
        here = (spot[0] * ny + spot[1]) * nz + spot[2]
        for f in range(6):
            d = f // 2
            there = here + (strides[d] if f % 2 else -strides[d])
            own = jnp.where(row == i * 6 + f, here, own)
            near = jnp.where(row == i * 6 + f, there, near)
            if f % 2:
                entry = jnp.where(spot[d] < grid[d] - 1, d * total + here, -1)
            else:
                entry = jnp.where(spot[d] > 0, d * total + there, -1)
            chosen = jnp.where(wide == i * 6 + f, entry, chosen)
        chosen = jnp.where(wide == faces + i, 3 * total + here, chosen)
    masks[...] = pick(jnp.where(across == chosen, 1.0, 0.0), pack_ref[...])
    difference = jnp.where(col == own, mode, 0.0) - jnp.where(col == near, mode, 0.0)
    difference = difference * masks[0:faces, 0:1]
    projector[...] = dot32(difference, inverse[...])

    begin = dot32(projector[...], floating * coarse_ref[...])
    search[...] = jnp.zeros_like(search)
    applied[...] = jnp.zeros_like(applied)
    resid[...] = jnp.zeros_like(resid)
    mult_ref[...] = jnp.zeros_like(mult_ref)
    source[...] = jnp.zeros_like(source)
    applied_source[...] = jnp.zeros_like(applied_source)
    face_sums[...] = jnp.zeros_like(face_sums)
    for i in range(block_x):
        for f in range(6):
            line_f = begin[i * 6 + f : i * 6 + f + 1]
            values = jnp.broadcast_to(line_f, (face, cases))
            fresh[i, f] = values
            load[i, f * face : (f + 1) * face] = values.astype(jnp.bfloat16)
            if f % 2:
                begin_ref[i, f // 2] = line_f

    pl.semaphore_wait(barrier, ny * nz + nx - 2)

    def remote(i, f):
        if f >= 2:
            return True
        return i == 0 if f == 0 else i == block_x - 1

    def has_near(f):
        return me[f // 2] < counts[f // 2] - 1 if f % 2 else me[f // 2] > 0

    def neighbour(f):
        return {AXES[f // 2]: me[f // 2] + (1 if f % 2 else -1)}

    def face_copy(slot, i, f, into):
        return pltpu.make_async_remote_copy(
            src_ref=trace.at[i, f],
            dst_ref=other.at[slot, into, f ^ 1],
            send_sem=send_sem.at[i * 6 + f],
            recv_sem=recv_sem.at[slot, into * 6 + (f ^ 1)],
            device_id=neighbour(f),
            device_id_type=MESH,
        )

    def send_face(slot, i, f):
        into = i
        if f < 2:
            into = 0 if f % 2 else block_x - 1
        return face_copy(slot, i, f, into)

    def arrival(slot, i, f):
        return pltpu.make_async_remote_copy(
            src_ref=trace.at[i, f],
            dst_ref=other.at[slot, i, f],
            send_sem=send_sem.at[i * 6 + f],
            recv_sem=recv_sem.at[slot, i * 6 + f],
            device_id=neighbour(f),
            device_id_type=MESH,
        )

    def sum_copy(f, g):
        return pltpu.make_async_remote_copy(
            src_ref=face_sums.at[f],
            dst_ref=near_sums.at[g],
            send_sem=ssend_sem.at[f],
            recv_sem=srecv_sem.at[g],
            device_id=neighbour(f),
            device_id_type=MESH,
        )

    plane = ny * nz
    place = (me[0] * ny + me[1]) * nz + me[2]
    own_rows = pl.ds(pl.multiple_of(place * block_rows, 8), block_rows)
    plane_rows = pl.ds(pl.multiple_of(me[0] * plane * block_rows, 8), plane * block_rows)

    def spread_out(slot, rows, peers, first):
        copies = []
        for number, target in peers:
            copy = pltpu.make_async_remote_copy(
                src_ref=gathered.at[slot, rows],
                dst_ref=gathered.at[slot, rows],
                send_sem=gsend_sem.at[slot, first + number],
                recv_sem=grecv_sem.at[slot, first + number],
                device_id=target,
                device_id_type=MESH,
            )
            copy.start()
            copies.append(copy)
        return copies

    def iterate(it, carry):
        before, curve = carry
        slot = lax.rem(it, 2)
        first = it == 0

        ww = jnp.zeros((1, cases), jnp.float32)
        wq = jnp.zeros((1, cases), jnp.float32)
        wt = jnp.zeros((1, cases), jnp.float32)
        pt = jnp.zeros((1, cases), jnp.float32)
        for d in (1, 2, 0):
            for f in (2 * d, 2 * d + 1):
                for i in range(block_x):

                    @pl.when(first)
                    def _():
                        flex_copy(i, f).wait()

                    trace[i, f] = jnp.dot(
                        flex[i, f * face : (f + 1) * face, :],
                        load[i],
                        preferred_element_type=jnp.float32,
                    )
                    if f % 2:

                        @pl.when(first)
                        def _():
                            if f == 3 and i == 0:
                                dual_copy.wait()
                            trace[i, f] = trace[i, f] - dual[i, f // 2]

                    face_sums[f, i : i + 1] = column_sums(trace[i, f])

                @pl.when(has_near(f))
                def _():
                    sum_copy(f, f ^ 1).start()
                    for i in range(block_x):
                        if f < 2 and remote(i, f) or f >= 2 and i == 0:
                            send_face(slot, i, f).start()

        for f in range(6):
            for i in range(block_x):
                values = trace[i, f]
                now = fresh[i, f]
                wt = wt + column_sums(now * values)
                pt = pt + column_sums(search[i, f] * values)
                if f % 2:
                    ww = ww + column_sums(now * now)
                    wq = wq + column_sums(now * applied[i, f])

        sources = [jnp.zeros((1, cases), jnp.float32) for _ in range(block_x)]
        for f in (2, 3, 4, 5, 0, 1):

            @pl.when(has_near(f))
            def _():
                sum_copy(f, f).wait_recv()

            for i in range(block_x):
                step = 1 if f % 2 else -1
                if f >= 2:
                    partner = near_sums[f, i : i + 1]
                elif remote(i, f):
                    k = block_x - 1 - i
                    partner = near_sums[f, k : k + 1]
                else:
                    partner = face_sums[f ^ 1, i + step : i + step + 1]
                row_of = i * 6 + f
                sources[i] = sources[i] + masks[row_of : row_of + 1, :] * (
                    face_sums[f, i : i + 1] - partner
                )
        lines = [
            sources[i] * (mode * masks[faces + i : faces + i + 1, :]) for i in range(block_x)
        ]
        lines = lines + [ww, wt, wq, pt]
        lines = lines + [jnp.zeros((1, cases), jnp.float32)] * (block_rows - len(lines))
        gathered[slot, own_rows] = jnp.concatenate(lines, axis=0)
        copies = spread_out(slot, own_rows, plane_peers(), 0)
        for f in (2, 3, 4, 5):

            @pl.when(has_near(f))
            def _():
                for i in range(1, block_x):
                    send_face(slot, i, f).start()

        for copy in copies:
            copy.wait_recv()
        lines_out = spread_out(slot, plane_rows, line_peers(), plane)
        for copy in lines_out:
            copy.wait_recv()

        ww, wt, wq, pt = [
            column_sums(gathered[slot, pl.ds(block_x + j, devices, stride=block_rows), :])
            for j in range(4)
        ]
        ratio = jnp.where(it <= 1, 0.0, ww / before)
        curve = wt + ratio * (wq + pt) + ratio * ratio * curve
        length = jnp.where(first, 1.0, ww / curve)
        for gx in range(nx):
            for i in range(block_x):
                at = (gx * block_x + i) * plane
                part = (
                    gathered[slot, pl.ds(gx * plane * block_rows + i, plane, stride=block_rows), :]
                    + ratio * applied_source[at : at + plane]
                )
                applied_source[at : at + plane] = part
                source[at : at + plane] = source[at : at + plane] - length * part
        spread = dot32(projector[...], source[...])
        moved = jnp.where(first, 0.0, length)

        for i in range(block_x):
            for f in (0, 1, 4, 5, 2, 3):
                if remote(i, f):

                    @pl.when(has_near(f))
                    def _():
                        arrival(slot, i, f).wait_recv()
                        send_face(slot, i, f).wait_send()

                    partner = other[slot, i, f]
                else:
                    partner = trace[i + (1 if f % 2 else -1), f ^ 1]
                row_of = i * 6 + f
                jump = masks[row_of : row_of + 1, :] * (trace[i, f] - partner)
                product = jump + ratio * applied[i, f]
                applied[i, f] = product
                toward = fresh[i, f] + ratio * search[i, f]
                search[i, f] = toward
                if f % 2:
                    mult_ref[i, f // 2] = mult_ref[i, f // 2] + moved * toward
                left = resid[i, f] - length * product
                resid[i, f] = left
                renewed = left - spread[row_of : row_of + 1]
                fresh[i, f] = renewed
                load[i, f * face : (f + 1) * face] = renewed.astype(jnp.bfloat16)
                if f % 2:
                    spread_ref[i, f // 2] = spread[row_of : row_of + 1]

        for f in range(6):

            @pl.when(has_near(f))
            def _():
                sum_copy(f, f ^ 1).wait_send()

        for copy in copies + lines_out:
            copy.wait_send()
        return ww, curve

    zero = jnp.zeros((1, cases), jnp.float32)
    lax.fori_loop(0, ITERS + 1, iterate, (zero, zero))
    for i in range(block_x):
        for d in range(3):
            out_ref[i, d] = resid[i, 2 * d + 1]


def per_device(counts, flexibility, dual_load, coarse_load, glue, floating_flag):
    block_x, block_y, block_z = dual_load.shape[:3]
    face, cases = dual_load.shape[4:]
    assert block_y == 1 and block_z == 1
    grid_x, grid_y, grid_z = floating_flag.shape
    total = grid_x * grid_y * grid_z
    nx, ny, nz = counts
    packed = jnp.concatenate([jnp.moveaxis(glue, 3, 0).reshape(3 * total), floating_flag.reshape(total)])
    packed = jnp.broadcast_to(packed.astype(jnp.float32)[:, None], (4 * total, cases))
    coarse = coarse_load.reshape(total, cases)
    block_rows = -(-(block_x + 4) // 8) * 8
    sum_rows = -(-block_x // 8) * 8
    mask_rows = -(-(block_x * 7) // 8) * 8
    devices = nx * ny * nz
    fields = (block_x, 6, face, cases)
    vmem = pl.BlockSpec(memory_space=pltpu.VMEM)
    hbm = pl.BlockSpec(memory_space=pl.ANY)
    out = jax.ShapeDtypeStruct((block_x, 3, face, cases), jnp.float32)
    small = jax.ShapeDtypeStruct((block_x, 3, 1, cases), jnp.float32)
    mult, resid, begin, spread = pl.pallas_call(
        functools.partial(kernel, counts, block_x, face),
        out_shape=(out, out, small, small),
        in_specs=[hbm, hbm, vmem, vmem],
        out_specs=(vmem, vmem, vmem, vmem),
        scratch_shapes=[
            pltpu.VMEM((block_x, 6 * face, 6 * face), jnp.bfloat16),
            pltpu.VMEM((block_x, 3, face, cases), jnp.float32),
            pltpu.VMEM((total, total), jnp.float32),
            pltpu.VMEM((6 * block_x, total), jnp.float32),
            pltpu.VMEM((mask_rows, cases), jnp.float32),
            pltpu.VMEM((block_x, 6 * face, cases), jnp.bfloat16),
            pltpu.VMEM(fields, jnp.float32),
            pltpu.VMEM((2,) + fields, jnp.float32),
            pltpu.VMEM(fields, jnp.float32),
            pltpu.VMEM(fields, jnp.float32),
            pltpu.VMEM(fields, jnp.float32),
            pltpu.VMEM(fields, jnp.float32),
            pltpu.VMEM((total, cases), jnp.float32),
            pltpu.VMEM((total, cases), jnp.float32),
            pltpu.VMEM((2, devices * block_rows, cases), jnp.float32),
            pltpu.VMEM((6, sum_rows, cases), jnp.float32),
            pltpu.VMEM((6, sum_rows, cases), jnp.float32),
            pltpu.SemaphoreType.DMA((6 * block_x,)),
            pltpu.SemaphoreType.DMA,
            pltpu.SemaphoreType.DMA((6 * block_x,)),
            pltpu.SemaphoreType.DMA((2, 6 * block_x)),
            pltpu.SemaphoreType.DMA((6,)),
            pltpu.SemaphoreType.DMA((6,)),
            pltpu.SemaphoreType.DMA((2, ny * nz + nx)),
            pltpu.SemaphoreType.DMA((2, ny * nz + nx)),
        ],
        compiler_params=pltpu.CompilerParams(collective_id=0, has_side_effects=True),
        name="feti_cg",
    )(
        flexibility.reshape(block_x, 6 * face, 6 * face),
        dual_load.reshape(block_x, 3, face, cases),
        coarse,
        packed,
    )
    shape = dual_load.shape
    return (mult + begin).reshape(shape), (resid - spread).reshape(shape)


def solution(mesh):
    counts = tuple(mesh.shape[axis] for axis in AXES)
    return jax.shard_map(
        functools.partial(per_device, counts),
        mesh=mesh,
        in_specs=(
            P("gx", "gy", "gz", None, None),
            P("gx", "gy", "gz", None, None, None),
            P(),
            P(),
            P(),
        ),
        out_specs=(P("gx", "gy", "gz", None, None, None), P("gx", "gy", "gz", None, None, None)),
        check_vma=False,
    )
```

```python
import functools
import math

import jax
import jax.numpy as jnp
from jax import lax
from jax.experimental import pallas as pl
from jax.experimental.pallas import tpu as pltpu
from jax.sharding import PartitionSpec as P

ITERS = 4
MESH = pl.DeviceIdType.MESH
AXES = ("gx", "gy", "gz")
HIGHEST = lax.Precision.HIGHEST


def dot32(left, right):
    return jnp.dot(left, right, precision=HIGHEST, preferred_element_type=jnp.float32)


def column_sums(values):
    return jnp.sum(values, axis=0, keepdims=True)


def kernel(
    counts,
    block_x,
    face,
    flex_hbm,
    dual_hbm,
    coarse_ref,
    pack_ref,
    mult_ref,
    out_ref,
    begin_ref,
    spread_ref,
    flex,
    dual,
    inverse,
    projector,
    masks,
    load,
    trace,
    other,
    fresh,
    search,
    resid,
    applied,
    source,
    applied_source,
    gathered,
    face_sums,
    near_sums,
    flex_sem,
    dual_sem,
    send_sem,
    recv_sem,
    ssend_sem,
    srecv_sem,
    gsend_sem,
    grecv_sem,
):
    nx, ny, nz = counts
    me = [lax.axis_index(axis) for axis in AXES]
    cases = coarse_ref.shape[1]
    total = coarse_ref.shape[0]
    grid = (nx * block_x, ny, nz)
    mode = 1.0 / math.sqrt(face)
    support = 2.0 / float(grid[0] * grid[0])
    block_rows = -(-(block_x + 4) // 8) * 8
    devices = nx * ny * nz
    faces = 6 * block_x
    strides = (ny * nz, nz, 1)

    def peer(axis, step):
        return lax.rem(me[axis] + step, counts[axis])

    def plane_peers():
        found = []
        for step_y in range(ny):
            for step_z in range(nz):
                if step_y or step_z:
                    target = {"gy": peer(1, step_y), "gz": peer(2, step_z)}
                    found.append((step_y * nz + step_z, target))
        return found

    def line_peers():
        return [(step, {"gx": peer(0, step)}) for step in range(1, nx)]

    def flex_copy(i, f):
        rows = pl.ds(f * face, face)
        return pltpu.make_async_copy(
            flex_hbm.at[i, rows], flex.at[i, rows], flex_sem.at[i * 6 + f]
        )

    dual_copy = pltpu.make_async_copy(dual_hbm, dual, dual_sem)
    for f in (2, 3, 4, 5, 0, 1):
        for i in range(block_x):
            flex_copy(i, f).start()
        if f == 2:
            dual_copy.start()

    other[...] = jnp.zeros_like(other)
    near_sums[...] = jnp.zeros_like(near_sums)
    barrier = pltpu.get_barrier_semaphore()
    for target in plane_peers() + line_peers():
        pl.semaphore_signal(barrier, inc=1, device_id=target[1], device_id_type=MESH)

    lane = lax.broadcasted_iota(jnp.int32, (total, total), 1)
    line = lax.broadcasted_iota(jnp.int32, (total, total), 0)
    lane_one = lax.broadcasted_iota(jnp.int32, (1, total), 1)
    tall = lax.broadcasted_iota(jnp.int32, (total, cases), 0)
    floating = pack_ref[3 * total : 4 * total, :]

    def pick(choice, values):
        return jnp.dot(choice, values, preferred_element_type=jnp.float32)

    degree = jnp.zeros((total, cases), jnp.float32)
    bands = jnp.zeros((total, total), jnp.float32)
    for d in range(3):
        place_d = lax.rem(lax.div(tall, strides[d]), grid[d])
        active = jnp.where(place_d < grid[d] - 1, pack_ref[d * total : (d + 1) * total, :], 0.0)
        above = jnp.where(lane == line + strides[d], 1.0, 0.0)
        below = jnp.where(lane == line - strides[d], 1.0, 0.0)
        active_below = pick(below, active)
        degree = degree + active + active_below
        link_above = active * floating * pick(above, floating)
        link_below = active_below * floating * pick(below, floating)
        bands = bands + above * link_above[:, 0:1] + below * link_below[:, 0:1]
    diagonal = jnp.where(floating > 0.0, degree + support, 1.0)
    inverse[...] = jnp.where(lane == line, diagonal[:, 0:1], 0.0) - bands

    def eliminate(k, carry):
        values = inverse[...]
        pivot_row = inverse[pl.ds(k, 1), :]
        pivot = jnp.sum(jnp.where(lane_one == k, pivot_row, 0.0), axis=1, keepdims=True)
        column = jnp.sum(jnp.where(lane == k, values, 0.0), axis=1, keepdims=True)
        scale = 1.0 / pivot
        scaled = jnp.where(lane_one == k, scale, pivot_row * scale)
        rest = jnp.where(lane == k, 0.0, values) - column * scaled
        inverse[...] = jnp.where(line == k, scaled, rest)
        return carry

    def eliminate_pair(half, carry):
        k = 2 * half
        values = inverse[...]
        rows = [inverse[pl.ds(k + j, 1), :] for j in range(2)]
        (a, b), (c, d) = [
            [
                jnp.sum(jnp.where(lane_one == k + j, pivot, 0.0), axis=1, keepdims=True)
                for j in range(2)
            ]
            for pivot in rows
        ]
        scale = 1.0 / (a * d - b * c)
        block = ((d * scale, -b * scale), (-c * scale, a * scale))
        rest = jnp.where(jnp.logical_or(lane == k, lane == k + 1), 0.0, values)
        results = []
        for j in range(2):
            column = jnp.sum(jnp.where(lane == k + j, values, 0.0), axis=1, keepdims=True)
            left, right = block[j]
            scaled = left * rows[0] + right * rows[1]
            scaled = jnp.where(lane_one == k, left, jnp.where(lane_one == k + 1, right, scaled))
            rest = rest - column * scaled
            results.append(scaled)
        rest = jnp.where(line == k, results[0], rest)
        inverse[...] = jnp.where(line == k + 1, results[1], rest)
        return carry

    if total % 2:
        lax.fori_loop(0, total, eliminate, 0)
    else:
        lax.fori_loop(0, total // 2, eliminate_pair, 0)

    mask_rows = masks.shape[0]
    wide = lax.broadcasted_iota(jnp.int32, (mask_rows, 4 * total), 0)
    across = lax.broadcasted_iota(jnp.int32, (mask_rows, 4 * total), 1)
    row = lax.broadcasted_iota(jnp.int32, (faces, total), 0)
    col = lax.broadcasted_iota(jnp.int32, (faces, total), 1)
    own = jnp.zeros((faces, total), jnp.int32)
    near = jnp.zeros((faces, total), jnp.int32)
    chosen = jnp.full((mask_rows, 4 * total), -1, jnp.int32)
    for i in range(block_x):
        spot = (me[0] * block_x + i, me[1], me[2])
        here = (spot[0] * ny + spot[1]) * nz + spot[2]
        for f in range(6):
            d = f // 2
            there = here + (strides[d] if f % 2 else -strides[d])
            own = jnp.where(row == i * 6 + f, here, own)
            near = jnp.where(row == i * 6 + f, there, near)
            if f % 2:
                entry = jnp.where(spot[d] < grid[d] - 1, d * total + here, -1)
            else:
                entry = jnp.where(spot[d] > 0, d * total + there, -1)
            chosen = jnp.where(wide == i * 6 + f, entry, chosen)
        chosen = jnp.where(wide == faces + i, 3 * total + here, chosen)
    masks[...] = pick(jnp.where(across == chosen, 1.0, 0.0), pack_ref[...])
    difference = jnp.where(col == own, mode, 0.0) - jnp.where(col == near, mode, 0.0)
    difference = difference * masks[0:faces, 0:1]
    projector[...] = dot32(difference, inverse[...])

    begin = dot32(projector[...], floating * coarse_ref[...])
    search[...] = jnp.zeros_like(search)
    applied[...] = jnp.zeros_like(applied)
    resid[...] = jnp.zeros_like(resid)
    mult_ref[...] = jnp.zeros_like(mult_ref)
    source[...] = jnp.zeros_like(source)
    applied_source[...] = jnp.zeros_like(applied_source)
    face_sums[...] = jnp.zeros_like(face_sums)
    for i in range(block_x):
        for f in range(6):
            line_f = begin[i * 6 + f : i * 6 + f + 1]
            values = jnp.broadcast_to(line_f, (face, cases))
            fresh[i, f] = values
            load[i, f * face : (f + 1) * face] = values.astype(jnp.bfloat16)
            if f % 2:
                begin_ref[i, f // 2] = line_f

    pl.semaphore_wait(barrier, ny * nz + nx - 2)

    def remote(i, f):
        if f >= 2:
            return True
        return i == 0 if f == 0 else i == block_x - 1

    def has_near(f):
        return me[f // 2] < counts[f // 2] - 1 if f % 2 else me[f // 2] > 0

    def neighbour(f):
        return {AXES[f // 2]: me[f // 2] + (1 if f % 2 else -1)}

    def face_copy(slot, i, f, into):
        return pltpu.make_async_remote_copy(
            src_ref=trace.at[i, f],
            dst_ref=other.at[slot, into, f ^ 1],
            send_sem=send_sem.at[i * 6 + f],
            recv_sem=recv_sem.at[slot, into * 6 + (f ^ 1)],
            device_id=neighbour(f),
            device_id_type=MESH,
        )

    def send_face(slot, i, f):
        into = i
        if f < 2:
            into = 0 if f % 2 else block_x - 1
        return face_copy(slot, i, f, into)

    def arrival(slot, i, f):
        return pltpu.make_async_remote_copy(
            src_ref=trace.at[i, f],
            dst_ref=other.at[slot, i, f],
            send_sem=send_sem.at[i * 6 + f],
            recv_sem=recv_sem.at[slot, i * 6 + f],
            device_id=neighbour(f),
            device_id_type=MESH,
        )

    def sum_copy(f, g):
        return pltpu.make_async_remote_copy(
            src_ref=face_sums.at[f],
            dst_ref=near_sums.at[g],
            send_sem=ssend_sem.at[f],
            recv_sem=srecv_sem.at[g],
            device_id=neighbour(f),
            device_id_type=MESH,
        )

    plane = ny * nz
    place = (me[0] * ny + me[1]) * nz + me[2]
    own_rows = pl.ds(pl.multiple_of(place * block_rows, 8), block_rows)
    plane_rows = pl.ds(pl.multiple_of(me[0] * plane * block_rows, 8), plane * block_rows)

    def spread_out(slot, rows, peers, first):
        copies = []
        for number, target in peers:
            copy = pltpu.make_async_remote_copy(
                src_ref=gathered.at[slot, rows],
                dst_ref=gathered.at[slot, rows],
                send_sem=gsend_sem.at[slot, first + number],
                recv_sem=grecv_sem.at[slot, first + number],
                device_id=target,
                device_id_type=MESH,
            )
            copy.start()
            copies.append(copy)
        return copies

    def iterate(it, carry):
        before, curve = carry
        slot = lax.rem(it, 2)
        first = it == 0

        ww = jnp.zeros((1, cases), jnp.float32)
        wq = jnp.zeros((1, cases), jnp.float32)
        wt = jnp.zeros((1, cases), jnp.float32)
        pt = jnp.zeros((1, cases), jnp.float32)
        for d in (1, 2, 0):
            for f in (2 * d, 2 * d + 1):
                for i in range(block_x):

                    @pl.when(first)
                    def _():
                        flex_copy(i, f).wait()

                    trace[i, f] = jnp.dot(
                        flex[i, f * face : (f + 1) * face, :],
                        load[i],
                        preferred_element_type=jnp.float32,
                    )
                    if f % 2:

                        @pl.when(first)
                        def _():
                            if f == 3 and i == 0:
                                dual_copy.wait()
                            trace[i, f] = trace[i, f] - dual[i, f // 2]

                    face_sums[f, i : i + 1] = column_sums(trace[i, f])

                @pl.when(has_near(f))
                def _():
                    sum_copy(f, f ^ 1).start()
                    for i in range(block_x):
                        if f < 2 and remote(i, f) or f >= 2 and i == 0:
                            send_face(slot, i, f).start()

        for f in range(6):
            for i in range(block_x):
                values = trace[i, f]
                now = fresh[i, f]
                wt = wt + column_sums(now * values)
                pt = pt + column_sums(search[i, f] * values)
                if f % 2:
                    ww = ww + column_sums(now * now)
                    wq = wq + column_sums(now * applied[i, f])

        sources = [jnp.zeros((1, cases), jnp.float32) for _ in range(block_x)]
        for f in (2, 3, 4, 5, 0, 1):

            @pl.when(has_near(f))
            def _():
                sum_copy(f, f).wait_recv()

            for i in range(block_x):
                step = 1 if f % 2 else -1
                if f >= 2:
                    partner = near_sums[f, i : i + 1]
                elif remote(i, f):
                    k = block_x - 1 - i
                    partner = near_sums[f, k : k + 1]
                else:
                    partner = face_sums[f ^ 1, i + step : i + step + 1]
                row_of = i * 6 + f
                sources[i] = sources[i] + masks[row_of : row_of + 1, :] * (
                    face_sums[f, i : i + 1] - partner
                )
        lines = [
            sources[i] * (mode * masks[faces + i : faces + i + 1, :]) for i in range(block_x)
        ]
        lines = lines + [ww, wt, wq, pt]
        lines = lines + [jnp.zeros((1, cases), jnp.float32)] * (block_rows - len(lines))
        gathered[slot, own_rows] = jnp.concatenate(lines, axis=0)
        copies = spread_out(slot, own_rows, plane_peers(), 0)
        for f in (2, 3, 4, 5):

            @pl.when(has_near(f))
            def _():
                for i in range(1, block_x):
                    send_face(slot, i, f).start()

        for copy in copies:
            copy.wait_recv()
        lines_out = spread_out(slot, plane_rows, line_peers(), plane)
        for copy in lines_out:
            copy.wait_recv()

        ww, wt, wq, pt = [
            column_sums(gathered[slot, pl.ds(block_x + j, devices, stride=block_rows), :])
            for j in range(4)
        ]
        ratio = jnp.where(it <= 1, 0.0, ww / before)
        curve = wt + ratio * (wq + pt) + ratio * ratio * curve
        length = jnp.where(first, 1.0, ww / curve)
        for gx in range(nx):
            for i in range(block_x):
                at = (gx * block_x + i) * plane
                part = (
                    gathered[slot, pl.ds(gx * plane * block_rows + i, plane, stride=block_rows), :]
                    + ratio * applied_source[at : at + plane]
                )
                applied_source[at : at + plane] = part
                source[at : at + plane] = source[at : at + plane] - length * part
        spread = dot32(projector[...], source[...])
        moved = jnp.where(first, 0.0, length)

        for i in range(block_x):
            for f in (0, 1, 4, 5, 2, 3):
                if remote(i, f):

                    @pl.when(has_near(f))
                    def _():
                        arrival(slot, i, f).wait_recv()
                        send_face(slot, i, f).wait_send()

                    partner = other[slot, i, f]
                else:
                    partner = trace[i + (1 if f % 2 else -1), f ^ 1]
                row_of = i * 6 + f
                jump = masks[row_of : row_of + 1, :] * (trace[i, f] - partner)
                product = jump + ratio * applied[i, f]
                applied[i, f] = product
                toward = fresh[i, f] + ratio * search[i, f]
                search[i, f] = toward
                if f % 2:
                    mult_ref[i, f // 2] = mult_ref[i, f // 2] + moved * toward
                left = resid[i, f] - length * product
                resid[i, f] = left
                renewed = left - spread[row_of : row_of + 1]
                fresh[i, f] = renewed
                load[i, f * face : (f + 1) * face] = renewed.astype(jnp.bfloat16)
                if f % 2:
                    spread_ref[i, f // 2] = spread[row_of : row_of + 1]

        for f in range(6):

            @pl.when(has_near(f))
            def _():
                sum_copy(f, f ^ 1).wait_send()

        for copy in copies + lines_out:
            copy.wait_send()
        return ww, curve

    zero = jnp.zeros((1, cases), jnp.float32)
    lax.fori_loop(0, ITERS + 1, iterate, (zero, zero))
    for i in range(block_x):
        for d in range(3):
            out_ref[i, d] = resid[i, 2 * d + 1]


def per_device(counts, flexibility, dual_load, coarse_load, glue, floating_flag):
    block_x, block_y, block_z = dual_load.shape[:3]
    face, cases = dual_load.shape[4:]
    assert block_y == 1 and block_z == 1
    grid_x, grid_y, grid_z = floating_flag.shape
    total = grid_x * grid_y * grid_z
    nx, ny, nz = counts
    packed = jnp.concatenate([jnp.moveaxis(glue, 3, 0).reshape(3 * total), floating_flag.reshape(total)])
    packed = jnp.broadcast_to(packed.astype(jnp.float32)[:, None], (4 * total, cases))
    coarse = coarse_load.reshape(total, cases)
    block_rows = -(-(block_x + 4) // 8) * 8
    sum_rows = -(-block_x // 8) * 8
    mask_rows = -(-(block_x * 7) // 8) * 8
    devices = nx * ny * nz
    fields = (block_x, 6, face, cases)
    vmem = pl.BlockSpec(memory_space=pltpu.VMEM)
    hbm = pl.BlockSpec(memory_space=pl.ANY)
    out = jax.ShapeDtypeStruct((block_x, 3, face, cases), jnp.float32)
    small = jax.ShapeDtypeStruct((block_x, 3, 1, cases), jnp.float32)
    mult, resid, begin, spread = pl.pallas_call(
        functools.partial(kernel, counts, block_x, face),
        out_shape=(out, out, small, small),
        in_specs=[hbm, hbm, vmem, vmem],
        out_specs=(vmem, vmem, vmem, vmem),
        scratch_shapes=[
            pltpu.VMEM((block_x, 6 * face, 6 * face), jnp.bfloat16),
            pltpu.VMEM((block_x, 3, face, cases), jnp.float32),
            pltpu.VMEM((total, total), jnp.float32),
            pltpu.VMEM((6 * block_x, total), jnp.float32),
            pltpu.VMEM((mask_rows, cases), jnp.float32),
            pltpu.VMEM((block_x, 6 * face, cases), jnp.bfloat16),
            pltpu.VMEM(fields, jnp.float32),
            pltpu.VMEM((2,) + fields, jnp.float32),
            pltpu.VMEM(fields, jnp.float32),
            pltpu.VMEM(fields, jnp.float32),
            pltpu.VMEM(fields, jnp.float32),
            pltpu.VMEM(fields, jnp.float32),
            pltpu.VMEM((total, cases), jnp.float32),
            pltpu.VMEM((total, cases), jnp.float32),
            pltpu.VMEM((2, devices * block_rows, cases), jnp.float32),
            pltpu.VMEM((6, sum_rows, cases), jnp.float32),
            pltpu.VMEM((6, sum_rows, cases), jnp.float32),
            pltpu.SemaphoreType.DMA((6 * block_x,)),
            pltpu.SemaphoreType.DMA,
            pltpu.SemaphoreType.DMA((6 * block_x,)),
            pltpu.SemaphoreType.DMA((2, 6 * block_x)),
            pltpu.SemaphoreType.DMA((6,)),
            pltpu.SemaphoreType.DMA((6,)),
            pltpu.SemaphoreType.DMA((2, ny * nz + nx)),
            pltpu.SemaphoreType.DMA((2, ny * nz + nx)),
        ],
        compiler_params=pltpu.CompilerParams(collective_id=0, has_side_effects=True),
        name="feti_cg",
    )(
        flexibility.reshape(block_x, 6 * face, 6 * face),
        dual_load.reshape(block_x, 3, face, cases),
        coarse,
        packed,
    )
    shape = dual_load.shape
    return (mult + begin).reshape(shape), (resid - spread).reshape(shape)


def solution(mesh):
    counts = tuple(mesh.shape[axis] for axis in AXES)
    return jax.shard_map(
        functools.partial(per_device, counts),
        mesh=mesh,
        in_specs=(
            P("gx", "gy", "gz", None, None),
            P("gx", "gy", "gz", None, None, None),
            P(),
            P(),
            P(),
        ),
        out_specs=(P("gx", "gy", "gz", None, None, None), P("gx", "gy", "gz", None, None, None)),
        check_vma=False,
    )
```
